512 devices in a mesh: node: 64 (over z_hi, y, core), local: 8 (over z_lo, x).
Axes of the slice: x: 4, y: 8, z: 8 (z_hi: 4, z_lo: 2; z = z_hi * 2 + z_lo), core: 2. Of those that a mesh axis runs over, the one named last changes fastest.
Arguments:
- block_input: bfloat16 [200704, 512], P(('node', 'local')), may hold values from 0 to 2
- conv_weight: bfloat16 [512, 2048], replicated, may hold values from -0.25 to 0.25
- bn_gain: float32 [2048], replicated, may hold values from 0.1 to 1.9
- out_cotangent: bfloat16 [200704, 2048], P(('node', 'local')), may hold values from -0.0546875 to 0.0546875
- master_weight: float32 [2048, 512], P('node'), may hold values from -0.25 to 0.25
- velocity: float32 [2048, 512], P('node'), may hold values from -6 to 6
Outputs:
- new_velocity: float32 [2048, 512], P('node')
- new_weight: float32 [2048, 512], P('node')
The draws below stay inside these ranges and needn't reach their ends.
All inputs are finite; a program needn't handle non-finite values.
Results may differ from the reference program's by a relative error of at most 0.0095.
Values may be sent and summed in bfloat16 or wider, within the bound.
A program may use at most 64 MiB of HBM per device.

```python
import jax
import jax.numpy as jnp
from jax import lax

CIN = 512
COUT = 2048
ROWS_DEV = 392
ROWS = 200704
DEVICES = 512


def spiked(values, stream_key, source, target, parts, factor):
    def block_of(dim):
        return (jnp.arange(values.shape[dim]) // (values.shape[dim] // parts)).reshape((-1,) + (1,) * (values.ndim - 1 - dim))

    first = jax.random.permutation(stream_key, parts)[block_of(target)]
    far = (block_of(target) + parts // 2) % parts
    return jnp.where((block_of(source) == first) | (block_of(source) == far), factor * values, values)


def steps_of(own_key, shape, split, least, largest):
    level, own = 1.0, jax.random.fold_in(own_key, 6)
    for position, blocks in split:
        heights = jnp.exp(jax.random.uniform(jax.random.fold_in(own, position), (blocks,), jnp.float32, least / len(split), largest / len(split)))
        level = level * jnp.repeat(heights, shape[position] // blocks).reshape([-1 if axis == position else 1 for axis in range(len(shape))])
    return level


def bell_draw(own_key, shape, scale, limit, split=(), dtype=jnp.bfloat16):
    values = jax.random.normal(own_key, shape, jnp.float32) * scale
    if len(split) > 0:
        values = steps_of(own_key, shape, split, -0.22, 0.18) * values
    return jnp.clip(values, min=-limit, max=limit).astype(dtype)


def noise_with(own_key, shape, width, reach, cuts, heavy, kind=jnp.bfloat16):
    entries = width * jax.random.normal(own_key, shape, jnp.float32)
    if cuts:
        entries = entries * steps_of(own_key, shape, cuts, -0.22, 0.18)
    return jnp.clip(spiked(entries, jax.random.fold_in(own_key, 3), *heavy), -reach, reach).astype(kind)


def setup_inputs(seed: int = 0) -> dict:
    keys = jax.random.split(jax.random.key(seed), 7)
    return {
        "block_input": jnp.clip(2.0 * jax.random.uniform(keys[0], (ROWS, CIN), jnp.float32) ** steps_of(keys[0], (ROWS, CIN), ((0, 512),), -0.2, 0.2), 0.0, 2.0).astype(jnp.bfloat16),
        "conv_weight": bell_draw(keys[1], (CIN, COUT), CIN ** -0.5, 0.25),
        "bn_gain": jnp.clip(1.0 + 0.18 * jax.random.normal(keys[2], (COUT,), jnp.float32), 0.1, 1.9),
        "out_cotangent": noise_with(keys[3], (ROWS, COUT), ((ROWS_DEV * DEVICES) ** -0.5), 0.0546875, ((0, 512),), (0, 1, 512, 6.0)),
        "master_weight": bell_draw(keys[4], (COUT, CIN), CIN ** -0.5, 0.25, ((0, 64),), jnp.float32),
        "velocity": bell_draw(keys[5], (COUT, CIN), 1.0, 6.0, ((0, 64),), jnp.float32),
    }


EPS = 1e-05
MOMENTUM = 0.9
RATE = 0.1
DECAY = 5e-05

def reference(block_input, conv_weight, bn_gain, out_cotangent, master_weight, velocity):
    inputs = block_input.reshape(DEVICES, ROWS_DEV, CIN)
    cotangents = out_cotangent.reshape(DEVICES, ROWS_DEV, COUT)

    def device_term(accumulated, pieces):
        activations, cotangent = pieces
        convolved = jnp.dot(activations, conv_weight, preferred_element_type=jnp.float32)
        center = lax.optimization_barrier(jnp.mean(convolved, axis=0))
        spread = convolved - center
        inverse = lax.rsqrt(lax.optimization_barrier(jnp.mean(spread * spread, axis=0)) + EPS)
        normed = spread * inverse
        upstream = cotangent.astype(jnp.float32)
        shift_grad = lax.optimization_barrier(jnp.sum(upstream, axis=0))
        gain_grad = lax.optimization_barrier(jnp.sum(upstream * normed, axis=0))
        conv_grad = (bn_gain * inverse / ROWS_DEV * (ROWS_DEV * upstream - shift_grad - normed * gain_grad)).astype(jnp.bfloat16)
        contribution = lax.dot_general(conv_grad, activations, (((0,), (0,)), ((), ())), preferred_element_type=jnp.float32)
        contribution = lax.optimization_barrier(contribution.astype(jnp.bfloat16)).astype(jnp.float32)
        return (accumulated + contribution, None)
    gradient, _ = lax.scan(device_term, jnp.zeros((COUT, CIN), jnp.float32), (inputs, cotangents))
    new_velocity = MOMENTUM * velocity + gradient + DECAY * master_weight
    new_weight = master_weight - RATE * new_velocity
    return (new_velocity, new_weight)
```

```python
import jax
import jax.numpy as jnp
from jax import lax
from jax.experimental import pallas as pl
from jax.experimental.pallas import tpu as pltpu
from jax.sharding import PartitionSpec as P

EPS = 1e-05
MOMENTUM = 0.9
RATE = 0.1
DECAY = 5e-05
MESH = pl.DeviceIdType.MESH
FAR_FIRST = (4, 3, 5, 2, 6, 1, 7)
F32 = jnp.float32
BF16 = jnp.bfloat16


def normalize_backward(block_input, conv_weight, bn_gain, out_cotangent):
    row_count = block_input.shape[0]
    convolved = jnp.dot(block_input, conv_weight, preferred_element_type=F32)
    center = jnp.mean(convolved, axis=0)
    spread = convolved - center
    inverse = lax.rsqrt(jnp.mean(spread * spread, axis=0) + EPS)
    normed = spread * inverse
    upstream = out_cotangent.astype(F32)
    shift_grad = jnp.sum(upstream, axis=0)
    gain_grad = jnp.sum(upstream * normed, axis=0)
    return (
        bn_gain * inverse / row_count * (row_count * upstream - shift_grad - normed * gain_grad)
    ).astype(BF16)


def reduce_kernel(
    term, out, pair_a, pair_b, mine_a, mine_b, ring_a, ring_b, part_a, part_b, last_a, last_b, piece, pieces,
    pair_send, pair_recv, ring_send, ring_recv, last_send, last_recv, piece_send, piece_recv,
):
    node = lax.axis_index("node")
    place = lax.axis_index("local")
    core = lax.rem(node, 2)
    y = lax.rem(node // 2, 8)
    z = (node // 16) * 2 + place // 4
    x = lax.rem(place, 4)

    def device(to_z, to_y, to_core):
        return ((to_z // 2) * 16 + to_y * 2 + to_core, lax.rem(to_z, 2) * 4 + x)

    def y_at(d):
        return device(z, lax.rem(y + d, 8), core)

    def z_at(d):
        return device(lax.rem(z + d, 8), y, core)

    def place_at(k):
        return (node, lax.rem(place + k, 8))

    partner = device(z, y, 1 - core)
    barrier = pltpu.get_barrier_semaphore()
    peers = [partner] + [y_at(d) for d in range(1, 8)] + [z_at(d) for d in range(1, 8)]
    peers += [place_at(k) for k in range(1, 8)]
    for peer in peers:
        pl.semaphore_signal(barrier, inc=1, device_id=peer, device_id_type=MESH)
    pl.semaphore_wait(barrier, len(peers))

    def send(source, target, sends, recvs, slot, peer):
        copy = pltpu.make_async_remote_copy(
            src_ref=source, dst_ref=target, send_sem=sends.at[slot], recv_sem=recvs.at[slot],
            device_id=peer, device_id_type=MESH,
        )
        copy.start()
        return copy

    left, right = pl.ds(0, 256), pl.ds(256, 256)
    started = []
    pairs = {}
    for d in FAR_FIRST + (0,):
        to_y = lax.rem(y + d, 8)
        to_z = lax.rem(z + d, 8)
        pairs["a", d] = send(
            term.at[:, to_y, 1 - core, :, :, left], pair_a.at[d], pair_send.at[0], pair_recv.at[0], d, partner
        )
        pairs["b", d] = send(
            term.at[to_z // 2, :, 1 - core, lax.rem(to_z, 2), :, right], pair_b.at[d],
            pair_send.at[1], pair_recv.at[1], d, partner,
        )
    rings = {}
    for d in FAR_FIRST + (0,):
        to_y = lax.rem(y + d, 8)
        to_z = lax.rem(z + d, 8)
        pairs["a", d].wait_recv()

        @pl.loop(0, 4)
        def _(i):
            own = term[i, to_y, core, :, :, 0:256].astype(F32)
            mine_a[d, i] = (own + pair_a[d, i].astype(F32)).astype(BF16)

        if d:
            rings["a", d] = send(mine_a.at[d], ring_a.at[d - 1], ring_send.at[0], ring_recv.at[0], d - 1, y_at(d))
        pairs["b", d].wait_recv()

        @pl.loop(0, 8)
        def _(i):
            own = term[to_z // 2, i, core, lax.rem(to_z, 2), :, 256:512].astype(F32)
            mine_b[d, i] = (own + pair_b[d, i].astype(F32)).astype(BF16)

        if d:
            rings["b", d] = send(mine_b.at[d], ring_b.at[d - 1], ring_send.at[1], ring_recv.at[1], d - 1, z_at(d))

    for d in range(1, 8):
        rings["a", d].wait_recv()

    @pl.loop(0, 8)
    def _(i):
        total = mine_a[0, i // 2, lax.rem(i, 2)].astype(F32)
        for d in range(7):
            total += ring_a[d, i // 2, lax.rem(i, 2)].astype(F32)
        part_a[i] = total.astype(BF16)

    lasts = {}
    for d in FAR_FIRST:
        lasts["a", d] = send(
            part_a.at[lax.rem(z + d, 8)], last_a.at[d - 1], last_send.at[0], last_recv.at[0], d - 1, z_at(d)
        )
    for d in range(1, 8):
        rings["b", d].wait_recv()

    @pl.loop(0, 8)
    def _(i):
        total = mine_b[0, i].astype(F32)
        for d in range(7):
            total += ring_b[d, i].astype(F32)
        part_b[i] = total.astype(BF16)

    for d in FAR_FIRST:
        lasts["b", d] = send(
            part_b.at[lax.rem(y + d, 8)], last_b.at[d - 1], last_send.at[1], last_recv.at[1], d - 1, y_at(d)
        )
    for d in range(1, 8):
        lasts["a", d].wait_recv()
    total = part_a[z].astype(F32)
    for d in range(7):
        total += last_a[d].astype(F32)
    piece[:, 0:256] = total.astype(BF16)
    for d in range(1, 8):
        lasts["b", d].wait_recv()
    total = part_b[y].astype(F32)
    for d in range(7):
        total += last_b[d].astype(F32)
    piece[:, 256:512] = total.astype(BF16)
    ends = [send(piece, pieces.at[place], piece_send, piece_recv, k - 1, place_at(k)) for k in range(1, 8)]
    pieces[place] = piece[...]
    for copy in ends:
        copy.wait_recv()
    for half in range(2):
        total = pieces[half * 4].astype(F32)
        for i in range(1, 4):
            total += pieces[half * 4 + i].astype(F32)
        out[half] = total
    for copy in [*pairs.values(), *rings.values(), *lasts.values(), *ends]:
        copy.wait_send()


def reduce_terms(term):
    dma = pltpu.SemaphoreType.DMA
    return pl.pallas_call(
        reduce_kernel,
        out_shape=jax.ShapeDtypeStruct((2, 16, 512), F32),
        in_specs=[pl.BlockSpec(memory_space=pltpu.VMEM)],
        out_specs=pl.BlockSpec(memory_space=pltpu.VMEM),
        scratch_shapes=[
            pltpu.VMEM((8, 4, 2, 16, 256), BF16),
            pltpu.VMEM((8, 8, 16, 256), BF16),
            pltpu.VMEM((8, 4, 2, 16, 256), BF16),
            pltpu.VMEM((8, 8, 16, 256), BF16),
            pltpu.VMEM((7, 4, 2, 16, 256), BF16),
            pltpu.VMEM((7, 8, 16, 256), BF16),
            pltpu.VMEM((8, 16, 256), BF16),
            pltpu.VMEM((8, 16, 256), BF16),
            pltpu.VMEM((7, 16, 256), BF16),
            pltpu.VMEM((7, 16, 256), BF16),
            pltpu.VMEM((16, 512), BF16),
            pltpu.VMEM((8, 16, 512), BF16),
            dma((2, 8)), dma((2, 8)), dma((2, 7)), dma((2, 7)), dma((2, 7)), dma((2, 7)), dma((7,)), dma((7,)),
        ],
        compiler_params=pltpu.CompilerParams(collective_id=0, has_side_effects=True),
    )(term)


def local(block_input, conv_weight, bn_gain, out_cotangent, master_weight, velocity):
    conv_grad = normalize_backward(block_input, conv_weight, bn_gain, out_cotangent)
    term = lax.dot_general(conv_grad, block_input, (((0,), (0,)), ((), ())), preferred_element_type=F32)
    term = term.astype(BF16).reshape(4, 8, 2, 2, 16, 512)
    gradient = reduce_terms(term).reshape(32, 512)
    new_velocity = MOMENTUM * velocity + gradient + DECAY * master_weight
    new_weight = master_weight - RATE * new_velocity
    return (new_velocity, new_weight)


def solution(mesh):
    in_specs = (
        P(("node", "local"), None),
        P(),
        P(),
        P(("node", "local"), None),
        P("node", None),
        P("node", None),
    )
    out_specs = (P("node", None), P("node", None))
    return jax.shard_map(local, mesh=mesh, in_specs=in_specs, out_specs=out_specs, check_vma=False)
```

```python
import jax
import jax.numpy as jnp
from jax import lax
from jax.experimental import pallas as pl
from jax.experimental.pallas import tpu as pltpu
from jax.sharding import PartitionSpec as P

EPS = 1e-05
MOMENTUM = 0.9
RATE = 0.1
DECAY = 5e-05
MESH = pl.DeviceIdType.MESH
FAR_FIRST = (4, 3, 5, 2, 6, 1, 7)
BLOCK_STEPS = (2, 1, 3, 0)
F32 = jnp.float32
BF16 = jnp.bfloat16
ROWS = 392
CIN = 512
WIDTH = 512


def conv_grad_of(x, weight, gain, cotangent):
    conv = jnp.dot(x, weight, preferred_element_type=F32)
    center = jnp.sum(conv, axis=0, keepdims=True) * (1.0 / ROWS)
    spread = conv - center
    inverse = lax.rsqrt(jnp.sum(spread * spread, axis=0, keepdims=True) * (1.0 / ROWS) + EPS)
    upstream = cotangent.astype(F32)
    shift_grad = jnp.sum(upstream, axis=0, keepdims=True)
    gain_grad = jnp.sum(upstream * spread, axis=0, keepdims=True) * inverse
    scale = gain * inverse / ROWS
    return (scale * (ROWS * upstream - shift_grad - spread * (inverse * gain_grad))).astype(BF16)


def step_kernel(
    x_hbm, weight_hbm, gain_hbm, cotangent_hbm, out, x, weight, gain, cotangent,
    term, pair, mine_a, mine_b, ring_a, ring_b, part_a, part_b, last_a, last_b, piece, pieces,
    x_sem, weight_sem, gain_sem, cotangent_sem, pair_send, pair_recv, ring_a_send, ring_a_recv, ring_b_send, ring_b_recv,
    last_send, last_recv, piece_send, piece_recv,
):
    node = lax.axis_index("node")
    place = lax.axis_index("local")
    core = lax.rem(node, 2)
    y = lax.rem(node // 2, 8)
    z_hi = node // 16
    z_lo = place // 4
    x_at = lax.rem(place, 4)
    high = [lax.rem(z_hi + step, 4) for step in BLOCK_STEPS]
    low = [z_lo, 1 - z_lo]

    def y_peer(d):
        return (z_hi * 16 + lax.rem(y + d, 8) * 2 + core, place)

    def z_peer(k, m):
        return (high[k] * 16 + y * 2 + core, low[m] * 4 + x_at)

    def place_peer(k):
        return (node, lax.rem(place + k, 8))

    partner = (node + 1 - 2 * core, place)
    z_slots = [(k, m) for k in range(4) for m in range(2) if (k, m) != (3, 0)]
    barrier = pltpu.get_barrier_semaphore()
    peers = [partner] + [y_peer(d) for d in range(1, 8)] + [z_peer(k, m) for k, m in z_slots]
    peers += [place_peer(k) for k in range(1, 8)]
    for peer in peers:
        pl.semaphore_signal(barrier, inc=1, device_id=peer, device_id_type=MESH)

    loads = [pltpu.make_async_copy(x_hbm, x, x_sem), pltpu.make_async_copy(gain_hbm, gain, gain_sem)]
    block_loads = []
    for k in range(4):
        columns = pl.ds(pl.multiple_of(high[k] * WIDTH, WIDTH), WIDTH)
        block_loads.append([
            pltpu.make_async_copy(weight_hbm.at[:, columns], weight.at[k], weight_sem.at[k]),
            pltpu.make_async_copy(cotangent_hbm.at[:, columns], cotangent.at[k], cotangent_sem.at[k]),
        ])
    for copy in [loads[0], *block_loads[0], loads[1], *block_loads[1], *block_loads[2], *block_loads[3]]:
        copy.start()

    def send(source, target, sends, recvs, peer):
        copy = pltpu.make_async_remote_copy(
            src_ref=source, dst_ref=target, send_sem=sends, recv_sem=recvs, device_id=peer, device_id_type=MESH
        )
        copy.start()
        return copy

    pairs, rings_a, rings_b, lasts, ends = {}, {}, {}, {}, []

    def compute(k):
        for copy in block_loads[k]:
            copy.wait()
        columns = pl.ds(pl.multiple_of(high[k] * WIDTH, WIDTH), WIDTH)
        grad = conv_grad_of(x[...], weight[k], gain[columns].reshape(1, WIDTH), cotangent[k])
        product = lax.dot_general(grad, x[...], (((0,), (0,)), ((), ())), preferred_element_type=F32)
        term[k] = product.astype(BF16).reshape(8, 2, 2, 16, CIN)

    def pair_up(k):
        pairs[k] = send(term.at[k, :, 1 - core], pair.at[k], pair_send.at[k], pair_recv.at[k], partner)

    def first_sums(k):
        pairs[k].wait_recv()

        @pl.loop(0, 8)
        def _(i):
            total = (term[k, i, core].astype(F32) + pair[k, i].astype(F32)).astype(BF16)
            mine_a[k, i] = total[:, :, 0:256]
            mine_b[k, 0, i] = total[0, :, 256:512]
            mine_b[k, 1, i] = total[1, :, 256:512]

        for d in FAR_FIRST:
            rings_a[k, d] = send(
                mine_a.at[k, lax.rem(y + d, 8)], ring_a.at[k, d - 1],
                ring_a_send.at[k, d - 1], ring_a_recv.at[k, d - 1], y_peer(d),
            )
        for m in range(2):
            if (k, m) in z_slots:
                slot = z_slots.index((k, m))
                rings_b[slot] = send(
                    mine_b.at[k, low[m]], ring_b.at[slot], ring_b_send.at[slot], ring_b_recv.at[slot], z_peer(k, m)
                )

    for copy in loads:
        copy.wait()
    for k in range(4):
        compute(k)
        if k == 0:
            pl.semaphore_wait(barrier, len(peers))
        pair_up(k)
        if k > 0:
            first_sums(k - 1)
    first_sums(3)

    for k in range(4):
        for d in range(1, 8):
            rings_a[k, d].wait_recv()
        total = mine_a[k, y].astype(F32)
        for d in range(7):
            total += ring_a[k, d].astype(F32)
        part_a[k] = total.astype(BF16)
        for m in range(2):
            if (k, m) in z_slots:
                slot = z_slots.index((k, m))
                lasts["a", slot] = send(
                    part_a.at[k, low[m]], last_a.at[slot], last_send.at[0, slot], last_recv.at[0, slot], z_peer(k, m)
                )
    for slot in range(7):
        rings_b[slot].wait_recv()

    @pl.loop(0, 8)
    def _(i):
        total = mine_b[3, z_lo, i].astype(F32)
        for slot in range(7):
            total += ring_b[slot, i].astype(F32)
        part_b[i] = total.astype(BF16)

    for d in FAR_FIRST:
        lasts["b", d - 1] = send(
            part_b.at[lax.rem(y + d, 8)], last_b.at[d - 1], last_send.at[1, d - 1], last_recv.at[1, d - 1], y_peer(d)
        )
    for slot in range(7):
        lasts["a", slot].wait_recv()
    total = part_a[3, z_lo].astype(F32)
    for slot in range(7):
        total += last_a[slot].astype(F32)
    piece[:, 0:256] = total.astype(BF16)
    for slot in range(7):
        lasts["b", slot].wait_recv()
    total = part_b[y].astype(F32)
    for slot in range(7):
        total += last_b[slot].astype(F32)
    piece[:, 256:512] = total.astype(BF16)
    for k in range(1, 8):
        ends.append(send(piece, pieces.at[place], piece_send.at[k - 1], piece_recv.at[k - 1], place_peer(k)))
    pieces[place] = piece[...]
    for copy in ends:
        copy.wait_recv()
    for half in range(2):
        total = pieces[half * 4].astype(F32)
        for i in range(1, 4):
            total += pieces[half * 4 + i].astype(F32)
        out[half] = total
    for copy in [*pairs.values(), *rings_a.values(), *rings_b.values(), *lasts.values(), *ends]:
        copy.wait_send()


def summed_gradient(block_input, conv_weight, bn_gain, out_cotangent):
    dma = pltpu.SemaphoreType.DMA
    return pl.pallas_call(
        step_kernel,
        out_shape=jax.ShapeDtypeStruct((2, 16, 512), F32),
        in_specs=[pl.BlockSpec(memory_space=pl.ANY)] * 4,
        out_specs=pl.BlockSpec(memory_space=pltpu.VMEM),
        scratch_shapes=[
            pltpu.VMEM((ROWS, CIN), BF16),
            pltpu.VMEM((4, CIN, WIDTH), BF16),
            pltpu.VMEM((4 * WIDTH,), F32),
            pltpu.VMEM((4, ROWS, WIDTH), BF16),
            pltpu.VMEM((4, 8, 2, 2, 16, CIN), BF16),
            pltpu.VMEM((4, 8, 2, 16, CIN), BF16),
            pltpu.VMEM((4, 8, 2, 16, 256), BF16),
            pltpu.VMEM((4, 2, 8, 16, 256), BF16),
            pltpu.VMEM((4, 7, 2, 16, 256), BF16),
            pltpu.VMEM((7, 8, 16, 256), BF16),
            pltpu.VMEM((4, 2, 16, 256), BF16),
            pltpu.VMEM((8, 16, 256), BF16),
            pltpu.VMEM((7, 16, 256), BF16),
            pltpu.VMEM((7, 16, 256), BF16),
            pltpu.VMEM((16, 512), BF16),
            pltpu.VMEM((8, 16, 512), BF16),
            dma, dma((4,)), dma, dma((4,)),
            dma((4,)), dma((4,)), dma((4, 7)), dma((4, 7)), dma((7,)), dma((7,)),
            dma((2, 7)), dma((2, 7)), dma((7,)), dma((7,)),
        ],
        compiler_params=pltpu.CompilerParams(collective_id=0, has_side_effects=True),
    )(block_input, conv_weight, bn_gain, out_cotangent)


def local(block_input, conv_weight, bn_gain, out_cotangent, master_weight, velocity):
    gradient = summed_gradient(block_input, conv_weight, bn_gain, out_cotangent).reshape(32, 512)
    new_velocity = MOMENTUM * velocity + gradient + DECAY * master_weight
    new_weight = master_weight - RATE * new_velocity
    return (new_velocity, new_weight)


def solution(mesh):
    in_specs = (
        P(("node", "local"), None),
        P(),
        P(),
        P(("node", "local"), None),
        P("node", None),
        P("node", None),
    )
    out_specs = (P("node", None), P("node", None))
    return jax.shard_map(local, mesh=mesh, in_specs=in_specs, out_specs=out_specs, check_vma=False)
```

```python
import jax
import jax.numpy as jnp
from jax import lax
from jax.experimental import pallas as pl
from jax.experimental.pallas import tpu as pltpu
from jax.sharding import PartitionSpec as P

EPS = 1e-05
MOMENTUM = 0.9
RATE = 0.1
DECAY = 5e-05
MESH = pl.DeviceIdType.MESH
FAR_FIRST = (4, 3, 5, 2, 6, 1, 7)
BLOCK_STEPS = (2, 1, 3, 0)
F32 = jnp.float32
BF16 = jnp.bfloat16
ROWS = 392
CIN = 512
WIDTH = 512


def conv_grad_of(x, weight, gain, cotangent):
    conv = jnp.dot(x, weight, preferred_element_type=F32)
    center = jnp.sum(conv, axis=0, keepdims=True) * (1.0 / ROWS)
    spread = conv - center
    inverse = lax.rsqrt(jnp.sum(spread * spread, axis=0, keepdims=True) * (1.0 / ROWS) + EPS)
    upstream = cotangent.astype(F32)
    shift_grad = jnp.sum(upstream, axis=0, keepdims=True)
    gain_grad = jnp.sum(upstream * spread, axis=0, keepdims=True) * inverse
    scale = gain * inverse / ROWS
    return (scale * (ROWS * upstream - shift_grad - spread * (inverse * gain_grad))).astype(BF16)


def step_kernel(
    x_hbm, weight_hbm, gain_hbm, cotangent_hbm, out, x, weight, gain, cotangent,
    term, pair, mine_a, mine_b, inbox_a, inbox_b, relay_a, relay_b, part_a, part_b, last_a, last_b, piece, pieces,
    x_sem, weight_sem, gain_sem, cotangent_sem, pair_send, pair_recv, a_send, a_recv, b_send, b_recv,
    last_send, last_recv, piece_send, piece_recv,
):
    node = lax.axis_index("node")
    place = lax.axis_index("local")
    core = lax.rem(node, 2)
    y = lax.rem(node // 2, 8)
    z_hi = node // 16
    z_lo = place // 4
    x_at = lax.rem(place, 4)
    high = [lax.rem(z_hi + step, 4) for step in BLOCK_STEPS]
    low = [z_lo, 1 - z_lo]
    z = z_hi * 2 + z_lo
    turn = 1 - 2 * core

    def y_peer(d):
        return (z_hi * 16 + lax.rem(y + d, 8) * 2 + core, place)

    def z_peer(k, m):
        return (high[k] * 16 + y * 2 + core, low[m] * 4 + x_at)

    def z_step(d):
        to_z = lax.rem(z + d + 8, 8)
        return ((to_z // 2) * 16 + y * 2 + core, lax.rem(to_z, 2) * 4 + x_at)

    def y_step(d):
        return lax.rem(y + d * turn + 8, 8)

    def place_peer(k):
        return (node, lax.rem(place + k, 8))

    partner = (node + 1 - 2 * core, place)
    z_slots = [(k, m) for k in range(4) for m in range(2) if (k, m) != (3, 0)]
    loads = [pltpu.make_async_copy(x_hbm, x, x_sem), pltpu.make_async_copy(gain_hbm, gain, gain_sem)]
    block_loads = []
    for k in range(4):
        columns = pl.ds(pl.multiple_of(high[k] * WIDTH, WIDTH), WIDTH)
        block_loads.append([
            pltpu.make_async_copy(weight_hbm.at[:, columns], weight.at[k], weight_sem.at[k]),
            pltpu.make_async_copy(cotangent_hbm.at[:, columns], cotangent.at[k], cotangent_sem.at[k]),
        ])
    for copy in [loads[0], *block_loads[0], loads[1], *block_loads[1], *block_loads[2], *block_loads[3]]:
        copy.start()

    barrier = pltpu.get_barrier_semaphore()
    peers = [partner] + [y_peer(d) for d in range(1, 8)] + [z_peer(k, m) for k, m in z_slots]
    peers += [place_peer(k) for k in range(1, 8)]
    for peer in peers:
        pl.semaphore_signal(barrier, inc=1, device_id=peer, device_id_type=MESH)

    def send(source, target, sends, recvs, peer):
        copy = pltpu.make_async_remote_copy(
            src_ref=source, dst_ref=target, send_sem=sends, recv_sem=recvs, device_id=peer, device_id_type=MESH
        )
        copy.start()
        return copy

    pairs, rings_a, rings_b, lasts, ends = {}, {}, {}, {}, []

    def compute(k):
        for copy in block_loads[k]:
            copy.wait()
        columns = pl.ds(pl.multiple_of(high[k] * WIDTH, WIDTH), WIDTH)
        grad = conv_grad_of(x[...], weight[k], gain[columns].reshape(1, WIDTH), cotangent[k])
        product = lax.dot_general(grad, x[...], (((0,), (0,)), ((), ())), preferred_element_type=F32)
        term[k] = product.astype(BF16).reshape(8, 2, 2, 16, CIN)

    def pair_up(k):
        pairs[k] = send(term.at[k, :, 1 - core], pair.at[k], pair_send.at[k], pair_recv.at[k], partner)

    def first_sums(k):
        pairs[k].wait_recv()

        @pl.loop(0, 8)
        def _(i):
            total = (term[k, i, core].astype(F32) + pair[k, i].astype(F32)).astype(BF16)
            mine_a[k, i] = total[:, :, 0:256]
            mine_b[k, 0, i] = total[0, :, 256:512]
            mine_b[k, 1, i] = total[1, :, 256:512]

        for slot, (hop, d) in enumerate(((2, 4), (1, 3), (-1, -3), (1, 1), (-1, -1))):
            send_a(k, slot, mine_a.at[k, y_step(d)], hop)
        if k == 0:
            send_b(0, mine_b.at[0, z_lo], 0, 2)
        if k < 3:
            slot, hop = ((2 - z_lo, 2 * z_lo - 1), (1 + 2 * z_lo, 1), (4 - 2 * z_lo, -1))[k]
        else:
            slot, hop = 3 + z_lo, 1 - 2 * z_lo
        send_b(1 + k, mine_b.at[k, 1 - z_lo], slot, hop)

    def send_a(k, slot, source, hop):
        rings_a[k, slot] = send(
            source, inbox_a.at[k, slot], a_send.at[k, slot], a_recv.at[k, slot],
            (z_hi * 16 + y_step(hop) * 2 + core, place),
        )

    def send_b(index, source, slot, hop):
        rings_b[index] = send(source, inbox_b.at[slot], b_send.at[index], b_recv.at[slot], z_step(hop))

    def got_a(k, slot):
        rings_a[k, slot].wait_recv()
        return inbox_a[k, slot].astype(F32)

    def relay_sums_a(k):
        relay_a[k, 0] = (mine_a[k, y_step(2)].astype(F32) + got_a(k, 0) + got_a(k, 1)).astype(BF16)
        send_a(k, 5, relay_a.at[k, 0], 2)
        relay_a[k, 1] = (mine_a[k, y_step(-2)].astype(F32) + got_a(k, 2)).astype(BF16)
        send_a(k, 6, relay_a.at[k, 1], -2)

    def wait_b(slot):
        pltpu.make_async_remote_copy(
            src_ref=inbox_b.at[slot], dst_ref=inbox_b.at[slot], send_sem=b_send.at[0], recv_sem=b_recv.at[slot],
            device_id=z_step(1), device_id_type=MESH,
        ).wait_recv()

    def relay_sums_b():
        wait_b(0)
        wait_b(1)

        @pl.loop(0, 8)
        def _(i):
            total = mine_b[1, z_lo, i].astype(F32) + inbox_b[0, i].astype(F32) + inbox_b[1, i].astype(F32)
            relay_b[0, i] = total.astype(BF16)

        send_b(5, relay_b.at[0], 5, 2)
        wait_b(2)

        @pl.loop(0, 8)
        def _(i):
            relay_b[1, i] = (mine_b[2, z_lo, i].astype(F32) + inbox_b[2, i].astype(F32)).astype(BF16)

        send_b(6, relay_b.at[1], 6, -2)

    def second_sums_a(k):
        total = mine_a[k, y].astype(F32)
        for slot in range(3, 7):
            total += got_a(k, slot)
        part_a[k] = total.astype(BF16)
        for m in range(2):
            if (k, m) in z_slots:
                slot = z_slots.index((k, m))
                lasts["a", slot] = send(
                    part_a.at[k, low[m]], last_a.at[slot], last_send.at[0, slot], last_recv.at[0, slot], z_peer(k, m)
                )

    def second_sums_b():
        for slot in range(3, 7):
            wait_b(slot)

        @pl.loop(0, 8)
        def _(i):
            total = mine_b[3, z_lo, i].astype(F32)
            for slot in range(3, 7):
                total += inbox_b[slot, i].astype(F32)
            part_b[i] = total.astype(BF16)

        for d in FAR_FIRST:
            lasts["b", d - 1] = send(
                part_b.at[lax.rem(y + d, 8)], last_b.at[d - 1], last_send.at[1, d - 1], last_recv.at[1, d - 1], y_peer(d)
            )

    for copy in loads:
        copy.wait()
    for k in range(4):
        compute(k)
        if k == 0:
            pl.semaphore_wait(barrier, len(peers))
        pair_up(k)
        if k > 0:
            first_sums(k - 1)
    relay_sums_a(0)
    relay_sums_a(1)
    first_sums(3)
    relay_sums_b()
    relay_sums_a(2)
    second_sums_a(0)
    second_sums_a(1)
    relay_sums_a(3)
    second_sums_b()
    second_sums_a(2)
    second_sums_a(3)
    for slot in range(7):
        lasts["a", slot].wait_recv()
    total = part_a[3, z_lo].astype(F32)
    for slot in range(7):
        total += last_a[slot].astype(F32)
    piece[:, 0:256] = total.astype(BF16)
    for slot in range(7):
        lasts["b", slot].wait_recv()
    total = part_b[y].astype(F32)
    for slot in range(7):
        total += last_b[slot].astype(F32)
    piece[:, 256:512] = total.astype(BF16)
    for k in range(1, 8):
        ends.append(send(piece, pieces.at[place], piece_send.at[k - 1], piece_recv.at[k - 1], place_peer(k)))
    pieces[place] = piece[...]
    for copy in ends:
        copy.wait_recv()
    for half in range(2):
        total = pieces[half * 4].astype(F32)
        for i in range(1, 4):
            total += pieces[half * 4 + i].astype(F32)
        out[half] = total
    for copy in [*pairs.values(), *rings_a.values(), *rings_b.values(), *lasts.values(), *ends]:
        copy.wait_send()


def summed_gradient(block_input, conv_weight, bn_gain, out_cotangent):
    dma = pltpu.SemaphoreType.DMA
    return pl.pallas_call(
        step_kernel,
        out_shape=pltpu.VMEM((2, 16, 512), F32),
        in_specs=[pl.BlockSpec(memory_space=pl.ANY)] * 4,
        out_specs=pl.BlockSpec(memory_space=pltpu.VMEM),
        scratch_shapes=[
            pltpu.VMEM((ROWS, CIN), BF16),
            pltpu.VMEM((4, CIN, WIDTH), BF16),
            pltpu.VMEM((4 * WIDTH,), F32),
            pltpu.VMEM((4, ROWS, WIDTH), BF16),
            pltpu.VMEM((4, 8, 2, 2, 16, CIN), BF16),
            pltpu.VMEM((4, 8, 2, 16, CIN), BF16),
            pltpu.VMEM((4, 8, 2, 16, 256), BF16),
            pltpu.VMEM((4, 2, 8, 16, 256), BF16),
            pltpu.VMEM((4, 7, 2, 16, 256), BF16),
            pltpu.VMEM((7, 8, 16, 256), BF16),
            pltpu.VMEM((4, 2, 2, 16, 256), BF16),
            pltpu.VMEM((2, 8, 16, 256), BF16),
            pltpu.VMEM((4, 2, 16, 256), BF16),
            pltpu.VMEM((8, 16, 256), BF16),
            pltpu.VMEM((7, 16, 256), BF16),
            pltpu.VMEM((7, 16, 256), BF16),
            pltpu.VMEM((16, 512), BF16),
            pltpu.VMEM((8, 16, 512), BF16),
            dma, dma((4,)), dma, dma((4,)),
            dma((4,)), dma((4,)), dma((4, 7)), dma((4, 7)), dma((7,)), dma((7,)),
            dma((2, 7)), dma((2, 7)), dma((7,)), dma((7,)),
        ],
        compiler_params=pltpu.CompilerParams(collective_id=0, has_side_effects=True),
    )(block_input, conv_weight, bn_gain, out_cotangent)


def local(block_input, conv_weight, bn_gain, out_cotangent, master_weight, velocity):
    gradient = summed_gradient(block_input, conv_weight, bn_gain, out_cotangent).reshape(32, 512)
    new_velocity = MOMENTUM * velocity + gradient + DECAY * master_weight
    new_weight = master_weight - RATE * new_velocity
    return (new_velocity, new_weight)


def solution(mesh):
    in_specs = (
        P(("node", "local"), None),
        P(),
        P(),
        P(("node", "local"), None),
        P("node", None),
        P("node", None),
    )
    out_specs = (P("node", None), P("node", None))
    return jax.shard_map(local, mesh=mesh, in_specs=in_specs, out_specs=out_specs, check_vma=False)
```

```python
import jax
import jax.numpy as jnp
from jax import lax
from jax.experimental import pallas as pl
from jax.experimental.pallas import tpu as pltpu
from jax.sharding import PartitionSpec as P

EPS = 1e-05
MOMENTUM = 0.9
RATE = 0.1
DECAY = 5e-05
MESH = pl.DeviceIdType.MESH
FAR_FIRST = (4, 3, 5, 2, 6, 1, 7)
BLOCK_STEPS = (2, 1, 3, 0)
F32 = jnp.float32
BF16 = jnp.bfloat16
ROWS = 392
CIN = 512
WIDTH = 512


def conv_grad_of(conv, gain, cotangent):
    center = jnp.sum(conv, axis=0, keepdims=True) * (1.0 / ROWS)
    spread = conv - center
    inverse = lax.rsqrt(jnp.sum(spread * spread, axis=0, keepdims=True) * (1.0 / ROWS) + EPS)
    upstream = cotangent.astype(F32)
    shift_grad = jnp.sum(upstream, axis=0, keepdims=True)
    gain_grad = jnp.sum(upstream * spread, axis=0, keepdims=True) * inverse
    scale = gain * inverse / ROWS
    return (scale * (ROWS * upstream - shift_grad - spread * (inverse * gain_grad))).astype(BF16)


def step_kernel(
    x_hbm, weight_hbm, gain_hbm, cotangent_hbm, out, x, weight, gain, cotangent,
    term, pair, mine_a, mine_b, inbox_a, inbox_b, relay_a, relay_b, part_a, part_b, last_a, last_b, piece, pieces,
    x_sem, weight_sem, gain_sem, cotangent_sem, pair_send, pair_recv, a_send, a_recv, b_send, b_recv,
    last_send, last_recv, piece_send, piece_recv,
):
    node = lax.axis_index("node")
    place = lax.axis_index("local")
    core = lax.rem(node, 2)
    y = lax.rem(node // 2, 8)
    z_hi = node // 16
    z_lo = place // 4
    x_at = lax.rem(place, 4)
    high = [lax.rem(z_hi + step, 4) for step in BLOCK_STEPS]
    low = [z_lo, 1 - z_lo]
    z = z_hi * 2 + z_lo
    turn = 1 - 2 * core
    apart = z_lo + core - 2 * z_lo * core

    def y_peer(d):
        return (z_hi * 16 + lax.rem(y + d, 8) * 2 + core, place)

    def z_peer(k, m):
        return (high[k] * 16 + y * 2 + core, low[m] * 4 + x_at)

    def z_step(d):
        to_z = lax.rem(z + d + 8, 8)
        return ((to_z // 2) * 16 + y * 2 + core, lax.rem(to_z, 2) * 4 + x_at)

    def y_step(d):
        return lax.rem(y + d * turn + 8, 8)

    def place_peer(k):
        return (node, lax.rem(place + k, 8))

    partner = (node + 1 - 2 * core, place)
    z_slots = [(k, m) for k in range(4) for m in range(2) if (k, m) != (3, 0)]
    loads = [pltpu.make_async_copy(x_hbm, x, x_sem), pltpu.make_async_copy(gain_hbm, gain, gain_sem)]
    block_loads = []
    for k in range(4):
        columns = pl.ds(pl.multiple_of(high[k] * WIDTH, WIDTH), WIDTH)
        block_loads.append([
            pltpu.make_async_copy(weight_hbm.at[:, columns], weight.at[k], weight_sem.at[k]),
            pltpu.make_async_copy(cotangent_hbm.at[:, columns], cotangent.at[k], cotangent_sem.at[k]),
        ])
    for copy in [loads[0], *block_loads[0], loads[1], *block_loads[1], *block_loads[2], *block_loads[3]]:
        copy.start()

    barrier = pltpu.get_barrier_semaphore()
    peers = [partner] + [y_peer(d) for d in range(1, 8)]
    peers += [z_step(d) for d in (1, -1, 2, -2)] + [place_peer(k) for k in range(1, 8)]
    for peer in peers:
        pl.semaphore_signal(barrier, inc=1, device_id=peer, device_id_type=MESH)

    def send(source, target, sends, recvs, peer):
        copy = pltpu.make_async_remote_copy(
            src_ref=source, dst_ref=target, send_sem=sends, recv_sem=recvs, device_id=peer, device_id_type=MESH
        )
        copy.start()
        return copy

    pairs, rings_a, rings_b, lasts, ends = {}, {}, {}, {}, []

    def conv_of(k):
        for copy in block_loads[k]:
            copy.wait()
        return jnp.dot(x[...], weight[k], preferred_element_type=F32)

    def finish(k, conv):
        columns = pl.ds(pl.multiple_of(high[k] * WIDTH, WIDTH), WIDTH)
        grad = conv_grad_of(conv, gain[columns].reshape(1, WIDTH), cotangent[k])
        product = lax.dot_general(grad, x[...], (((0,), (0,)), ((), ())), preferred_element_type=F32)
        term[k] = product.astype(BF16).reshape(8, 2, 2, 16, CIN)

    def pair_up(k):
        pairs[k] = send(term.at[k, :, 1 - core], pair.at[k], pair_send.at[k], pair_recv.at[k], partner)

    def first_sums(k):
        pairs[k].wait_recv()

        for i in range(8):
            total = (term[k, i, core].astype(F32) + pair[k, i].astype(F32)).astype(BF16)
            mine_a[k, i] = total[:, :, 0:256]
            mine_b[k, 0, i] = total[0, :, 256:512]
            mine_b[k, 1, i] = total[1, :, 256:512]

        if k < 3:
            for slot, (hop, d) in enumerate(((2, 4), (1, 3), (-1, -3), (1, 1), (-1, -1))):
                send_a(k, slot, mine_a.at[k, y_step(d)], hop)
        else:
            for slot, d in enumerate((4, 3, -3, 2, -2, 1, -1)):
                send_a(k, slot, mine_a.at[k, y_step(d)], d)
        if k == 0:
            send_b(0, mine_b.at[0, z_lo], 0, 2 * turn)
        slot, hop = (
            (2 - apart, 2 * z_lo - 1), (1 + 2 * z_lo + core, 1), (4 - 2 * z_lo - core, -1), (3 + apart, 1 - 2 * z_lo)
        )[k]
        send_b(1 + k, mine_b.at[k, 1 - z_lo], slot, hop)

    def send_a(k, slot, source, hop):
        rings_a[k, slot] = send(
            source, inbox_a.at[k, slot], a_send.at[k, slot], a_recv.at[k, slot],
            (z_hi * 16 + y_step(hop) * 2 + core, place),
        )

    def send_b(index, source, slot, hop):
        rings_b[index] = send(source, inbox_b.at[slot], b_send.at[index], b_recv.at[slot], z_step(hop))

    def got_a(k, slot):
        rings_a[k, slot].wait_recv()
        return inbox_a[k, slot].astype(F32)

    def relay_sums_a(k):
        relay_a[k, 0] = (mine_a[k, y_step(2)].astype(F32) + got_a(k, 0) + got_a(k, 1)).astype(BF16)
        send_a(k, 5, relay_a.at[k, 0], 2)
        relay_a[k, 1] = (mine_a[k, y_step(-2)].astype(F32) + got_a(k, 2)).astype(BF16)
        send_a(k, 6, relay_a.at[k, 1], -2)

    def wait_b(slot):
        pltpu.make_async_remote_copy(
            src_ref=inbox_b.at[slot], dst_ref=inbox_b.at[slot], send_sem=b_send.at[0], recv_sem=b_recv.at[slot],
            device_id=z_step(1), device_id_type=MESH,
        ).wait_recv()

    def relay_sums_b():
        wait_b(0)
        wait_b(1)

        for i in range(8):
            total = mine_b[1 + core, z_lo, i].astype(F32) + inbox_b[0, i].astype(F32) + inbox_b[1, i].astype(F32)
            relay_b[0, i] = total.astype(BF16)

        send_b(5, relay_b.at[0], 5, 2 * turn)
        wait_b(2)

        for i in range(8):
            relay_b[1, i] = (mine_b[2 - core, z_lo, i].astype(F32) + inbox_b[2, i].astype(F32)).astype(BF16)

        send_b(6, relay_b.at[1], 6, -2 * turn)

    def second_sums_a(k):
        total = mine_a[k, y].astype(F32)
        for slot in range(3 if k < 3 else 0, 7):
            total += got_a(k, slot)
        part_a[k] = total.astype(BF16)
        for m in range(2):
            if (k, m) in z_slots:
                slot = z_slots.index((k, m))
                lasts["a", slot] = send(
                    part_a.at[k, low[m]], last_a.at[slot], last_send.at[0, slot], last_recv.at[0, slot], z_peer(k, m)
                )

    def second_sums_b():
        for slot in range(3, 7):
            wait_b(slot)

        for i in range(8):
            total = mine_b[3, z_lo, i].astype(F32)
            for slot in range(3, 7):
                total += inbox_b[slot, i].astype(F32)
            part_b[i] = total.astype(BF16)

        for d in FAR_FIRST:
            lasts["b", d - 1] = send(
                part_b.at[lax.rem(y + d, 8)], last_b.at[d - 1], last_send.at[1, d - 1], last_recv.at[1, d - 1], y_peer(d)
            )

    def send_pieces():
        for k in range(1, 8):
            ends.append(send(
                piece, pieces.at[place],
                piece_send.at[0, k - 1], piece_recv.at[0, k - 1], place_peer(k),
            ))

    for copy in loads:
        copy.wait()
    conv = conv_of(0)
    for k in range(4):
        following = conv_of(k + 1) if k < 3 else None
        finish(k, conv)
        conv = following
        if k == 0:
            pl.semaphore_wait(barrier, len(peers))
        pair_up(k)
        if k > 0:
            first_sums(k - 1)
    first_sums(3)
    relay_sums_a(0)
    relay_sums_a(1)
    relay_sums_b()
    relay_sums_a(2)
    second_sums_a(0)
    second_sums_a(1)
    second_sums_b()
    second_sums_a(2)
    second_sums_a(3)
    for slot in range(7):
        lasts["a", slot].wait_recv()
    total = part_a[3, z_lo].astype(F32)
    for slot in range(7):
        total += last_a[slot].astype(F32)
    piece[:, 0:256] = total.astype(BF16)
    for slot in range(7):
        lasts["b", slot].wait_recv()
    total = part_b[y].astype(F32)
    for slot in range(7):
        total += last_b[slot].astype(F32)
    piece[:, 256:512] = total.astype(BF16)
    send_pieces()
    pieces[place] = piece[...]
    for copy in ends:
        copy.wait_recv()
    for half in range(2):
        total = pieces[half * 4].astype(F32)
        for i in range(1, 4):
            total += pieces[half * 4 + i].astype(F32)
        out[half] = total
    for copy in [*pairs.values(), *rings_a.values(), *rings_b.values(), *lasts.values(), *ends]:
        copy.wait_send()


def summed_gradient(block_input, conv_weight, bn_gain, out_cotangent):
    dma = pltpu.SemaphoreType.DMA
    return pl.pallas_call(
        step_kernel,
        out_shape=pltpu.VMEM((2, 16, 512), F32),
        in_specs=[pl.BlockSpec(memory_space=pl.ANY)] * 4,
        out_specs=pl.BlockSpec(memory_space=pltpu.VMEM),
        scratch_shapes=[
            pltpu.VMEM((ROWS, CIN), BF16),
            pltpu.VMEM((4, CIN, WIDTH), BF16),
            pltpu.VMEM((4 * WIDTH,), F32),
            pltpu.VMEM((4, ROWS, WIDTH), BF16),
            pltpu.VMEM((4, 8, 2, 2, 16, CIN), BF16),
            pltpu.VMEM((4, 8, 2, 16, CIN), BF16),
            pltpu.VMEM((4, 8, 2, 16, 256), BF16),
            pltpu.VMEM((4, 2, 8, 16, 256), BF16),
            pltpu.VMEM((4, 7, 2, 16, 256), BF16),
            pltpu.VMEM((7, 8, 16, 256), BF16),
            pltpu.VMEM((4, 2, 2, 16, 256), BF16),
            pltpu.VMEM((2, 8, 16, 256), BF16),
            pltpu.VMEM((4, 2, 16, 256), BF16),
            pltpu.VMEM((8, 16, 256), BF16),
            pltpu.VMEM((7, 16, 256), BF16),
            pltpu.VMEM((7, 16, 256), BF16),
            pltpu.VMEM((16, 512), BF16),
            pltpu.VMEM((8, 16, 512), BF16),
            dma, dma((4,)), dma, dma((4,)),
            dma((4,)), dma((4,)), dma((4, 7)), dma((4, 7)), dma((7,)), dma((7,)),
            dma((2, 7)), dma((2, 7)), dma((2, 7)), dma((2, 7)),
        ],
        compiler_params=pltpu.CompilerParams(collective_id=0, has_side_effects=True),
    )(block_input, conv_weight, bn_gain, out_cotangent)


def local(block_input, conv_weight, bn_gain, out_cotangent, master_weight, velocity):
    gradient = summed_gradient(block_input, conv_weight, bn_gain, out_cotangent).reshape(32, 512)
    new_velocity = MOMENTUM * velocity + gradient + DECAY * master_weight
    new_weight = master_weight - RATE * new_velocity
    return (new_velocity, new_weight)


def solution(mesh):
    in_specs = (
        P(("node", "local"), None),
        P(),
        P(),
        P(("node", "local"), None),
        P("node", None),
        P("node", None),
    )
    out_specs = (P("node", None), P("node", None))
    return jax.shard_map(local, mesh=mesh, in_specs=in_specs, out_specs=out_specs, check_vma=False)
```

```python
import jax
import jax.numpy as jnp
from jax import lax
from jax.experimental import pallas as pl
from jax.experimental.pallas import tpu as pltpu
from jax.sharding import PartitionSpec as P

EPS = 1e-05
MOMENTUM = 0.9
RATE = 0.1
DECAY = 5e-05
MESH = pl.DeviceIdType.MESH
FAR_FIRST = (4, 3, 5, 2, 6, 1, 7)
BLOCK_STEPS = (2, 1, 3, 0)
F32 = jnp.float32
BF16 = jnp.bfloat16
ROWS = 392
CIN = 512
WIDTH = 512


def conv_grad_of(conv, gain, cotangent):
    center = jnp.sum(conv, axis=0, keepdims=True) * (1.0 / ROWS)
    spread = conv - center
    inverse = lax.rsqrt(jnp.sum(spread * spread, axis=0, keepdims=True) * (1.0 / ROWS) + EPS)
    upstream = cotangent.astype(F32)
    shift_grad = jnp.sum(upstream, axis=0, keepdims=True)
    gain_grad = jnp.sum(upstream * spread, axis=0, keepdims=True) * inverse
    scale = gain * inverse / ROWS
    return (scale * (ROWS * upstream - shift_grad - spread * (inverse * gain_grad))).astype(BF16)


def step_kernel(
    x_hbm, weight_hbm, gain_hbm, cotangent_hbm, out, x, weight, gain, cotangent,
    term, pair, mine_a, mine_b, inbox_a, inbox_b, relay_a, relay_b, part_a, part_b, last_a, last_b, piece, pieces,
    x_sem, weight_sem, gain_sem, cotangent_sem, pair_send, pair_recv, a_send, a_recv, b_send, b_recv,
    last_send, last_recv, piece_send, piece_recv,
):
    node = lax.axis_index("node")
    place = lax.axis_index("local")
    core = lax.rem(node, 2)
    y = lax.rem(node // 2, 8)
    z_hi = node // 16
    z_lo = place // 4
    x_at = lax.rem(place, 4)
    high = [lax.rem(z_hi + step, 4) for step in BLOCK_STEPS]
    low = [z_lo, 1 - z_lo]
    z = z_hi * 2 + z_lo
    turn = 1 - 2 * core
    apart = z_lo + core - 2 * z_lo * core

    def y_peer(d):
        return (z_hi * 16 + lax.rem(y + d, 8) * 2 + core, place)

    def z_peer(k, m):
        return (high[k] * 16 + y * 2 + core, low[m] * 4 + x_at)

    def z_step(d):
        to_z = lax.rem(z + d + 8, 8)
        return ((to_z // 2) * 16 + y * 2 + core, lax.rem(to_z, 2) * 4 + x_at)

    def y_step(d):
        return lax.rem(y + d * turn + 8, 8)

    def place_peer(k):
        return (node, lax.rem(place + k, 8))

    partner = (node + 1 - 2 * core, place)
    z_slots = [(k, m) for k in range(4) for m in range(2) if (k, m) != (3, 0)]
    loads = [pltpu.make_async_copy(x_hbm, x, x_sem), pltpu.make_async_copy(gain_hbm, gain, gain_sem)]
    block_loads = []
    for k in range(4):
        columns = pl.ds(pl.multiple_of(high[k] * WIDTH, WIDTH), WIDTH)
        block_loads.append([
            pltpu.make_async_copy(weight_hbm.at[:, columns], weight.at[k], weight_sem.at[k]),
            pltpu.make_async_copy(cotangent_hbm.at[:, columns], cotangent.at[k], cotangent_sem.at[k]),
        ])
    for copy in [loads[0], *block_loads[0], loads[1]]:
        copy.start()

    barrier = pltpu.get_barrier_semaphore()
    peers = [partner] + [y_peer(d) for d in range(1, 8)]
    peers += [z_step(d) for d in (1, -1, 2, -2)] + [place_peer(k) for k in range(1, 8)]
    for peer in peers:
        pl.semaphore_signal(barrier, inc=1, device_id=peer, device_id_type=MESH)
    for copy in [*block_loads[1], *block_loads[2], *block_loads[3]]:
        copy.start()

    def send(source, target, sends, recvs, peer):
        copy = pltpu.make_async_remote_copy(
            src_ref=source, dst_ref=target, send_sem=sends, recv_sem=recvs, device_id=peer, device_id_type=MESH
        )
        copy.start()
        return copy

    pairs, rings_a, rings_b, lasts, ends = {}, {}, {}, {}, []

    def conv_of(k):
        for copy in block_loads[k]:
            copy.wait()
        return jnp.dot(x[...], weight[k], preferred_element_type=F32)

    def finish(k, conv):
        columns = pl.ds(pl.multiple_of(high[k] * WIDTH, WIDTH), WIDTH)
        grad = conv_grad_of(conv, gain[columns].reshape(1, WIDTH), cotangent[k])
        product = lax.dot_general(grad, x[...], (((0,), (0,)), ((), ())), preferred_element_type=F32)
        term[k] = product.astype(BF16).reshape(8, 2, 2, 16, CIN)

    def pair_up(k):
        pairs[k] = send(term.at[k, :, 1 - core], pair.at[k], pair_send.at[k], pair_recv.at[k], partner)

    def first_sums(k):
        pairs[k].wait_recv()

        for i in range(8):
            total = (term[k, i, core].astype(F32) + pair[k, i].astype(F32)).astype(BF16)
            mine_a[k, i] = total[:, :, 0:256]
            mine_b[k, 0, i] = total[0, :, 256:512]
            mine_b[k, 1, i] = total[1, :, 256:512]

        if k < 3:
            for slot, (hop, d) in enumerate(((2, 4), (1, 3), (-1, -3), (1, 1), (-1, -1))):
                send_a(k, slot, mine_a.at[k, y_step(d)], hop)
        else:
            for slot, d in enumerate((4, 3, -3, 2, -2, 1, -1)):
                send_a(k, slot, mine_a.at[k, y_step(d)], d)
        if k == 0:
            send_b(0, mine_b.at[0, z_lo], 0, 2 * turn)
        slot, hop = (
            (2 - apart, 2 * z_lo - 1), (1 + 2 * z_lo + core, 1), (4 - 2 * z_lo - core, -1), (3 + apart, 1 - 2 * z_lo)
        )[k]
        send_b(1 + k, mine_b.at[k, 1 - z_lo], slot, hop)

    def send_a(k, slot, source, hop):
        rings_a[k, slot] = send(
            source, inbox_a.at[k, slot], a_send.at[k, slot], a_recv.at[k, slot],
            (z_hi * 16 + y_step(hop) * 2 + core, place),
        )

    def send_b(index, source, slot, hop):
        rings_b[index] = send(source, inbox_b.at[slot], b_send.at[index], b_recv.at[slot], z_step(hop))

    def got_a(k, slot):
        rings_a[k, slot].wait_recv()
        return inbox_a[k, slot].astype(F32)

    def relay_sums_a(k):
        relay_a[k, 0] = (mine_a[k, y_step(2)].astype(F32) + got_a(k, 0) + got_a(k, 1)).astype(BF16)
        send_a(k, 5, relay_a.at[k, 0], 2)
        relay_a[k, 1] = (mine_a[k, y_step(-2)].astype(F32) + got_a(k, 2)).astype(BF16)
        send_a(k, 6, relay_a.at[k, 1], -2)

    def wait_b(slot):
        pltpu.make_async_remote_copy(
            src_ref=inbox_b.at[slot], dst_ref=inbox_b.at[slot], send_sem=b_send.at[0], recv_sem=b_recv.at[slot],
            device_id=z_step(1), device_id_type=MESH,
        ).wait_recv()

    def relay_sums_b():
        wait_b(0)
        wait_b(1)

        for i in range(8):
            total = mine_b[1 + core, z_lo, i].astype(F32) + inbox_b[0, i].astype(F32) + inbox_b[1, i].astype(F32)
            relay_b[0, i] = total.astype(BF16)

        send_b(5, relay_b.at[0], 5, 2 * turn)
        wait_b(2)

        for i in range(8):
            relay_b[1, i] = (mine_b[2 - core, z_lo, i].astype(F32) + inbox_b[2, i].astype(F32)).astype(BF16)

        send_b(6, relay_b.at[1], 6, -2 * turn)

    def second_sums_a(k):
        total = mine_a[k, y].astype(F32)
        for slot in range(3 if k < 3 else 0, 7):
            total += got_a(k, slot)
        part_a[k] = total.astype(BF16)
        for m in range(2):
            if (k, m) in z_slots:
                slot = z_slots.index((k, m))
                lasts["a", slot] = send(
                    part_a.at[k, low[m]], last_a.at[slot], last_send.at[0, slot], last_recv.at[0, slot], z_peer(k, m)
                )

    def second_sums_b():
        for slot in range(3, 7):
            wait_b(slot)

        for i in range(8):
            total = mine_b[3, z_lo, i].astype(F32)
            for slot in range(3, 7):
                total += inbox_b[slot, i].astype(F32)
            part_b[i] = total.astype(BF16)

        for d in FAR_FIRST:
            lasts["b", d - 1] = send(
                part_b.at[lax.rem(y + d, 8)], last_b.at[d - 1], last_send.at[1, d - 1], last_recv.at[1, d - 1], y_peer(d)
            )

    def send_pieces():
        for k in (2, 6, 1, 3, 5, 7, 4):
            ends.append(send(
                piece, pieces.at[place],
                piece_send.at[0, k - 1], piece_recv.at[0, k - 1], place_peer(k),
            ))

    for copy in loads:
        copy.wait()
    conv = conv_of(0)
    for k in range(4):
        following = conv_of(k + 1) if k < 3 else None
        finish(k, conv)
        conv = following
        if k == 0:
            pl.semaphore_wait(barrier, len(peers))
        pair_up(k)
        if k > 0:
            first_sums(k - 1)
    first_sums(3)
    relay_sums_b()
    relay_sums_a(0)
    relay_sums_a(1)
    relay_sums_a(2)
    second_sums_a(0)
    second_sums_a(1)
    second_sums_b()
    second_sums_a(2)
    second_sums_a(3)
    for slot in range(7):
        lasts["a", slot].wait_recv()
    total = part_a[3, z_lo].astype(F32)
    for slot in range(7):
        total += last_a[slot].astype(F32)
    piece[:, 0:256] = total.astype(BF16)
    for slot in range(7):
        lasts["b", slot].wait_recv()
    total = part_b[y].astype(F32)
    for slot in range(7):
        total += last_b[slot].astype(F32)
    piece[:, 256:512] = total.astype(BF16)
    send_pieces()
    pieces[place] = piece[...]
    for copy in [*pairs.values(), *rings_a.values(), *rings_b.values(), *lasts.values()]:
        copy.wait_send()
    for copy in ends:
        copy.wait_recv()
    for half in range(2):
        total = pieces[half * 4].astype(F32)
        for i in range(1, 4):
            total += pieces[half * 4 + i].astype(F32)
        out[half] = total
    for copy in ends:
        copy.wait_send()


def summed_gradient(block_input, conv_weight, bn_gain, out_cotangent):
    dma = pltpu.SemaphoreType.DMA
    return pl.pallas_call(
        step_kernel,
        out_shape=pltpu.VMEM((2, 16, 512), F32),
        in_specs=[pl.BlockSpec(memory_space=pl.ANY)] * 4,
        out_specs=pl.BlockSpec(memory_space=pltpu.VMEM),
        scratch_shapes=[
            pltpu.VMEM((ROWS, CIN), BF16),
            pltpu.VMEM((4, CIN, WIDTH), BF16),
            pltpu.VMEM((4 * WIDTH,), F32),
            pltpu.VMEM((4, ROWS, WIDTH), BF16),
            pltpu.VMEM((4, 8, 2, 2, 16, CIN), BF16),
            pltpu.VMEM((4, 8, 2, 16, CIN), BF16),
            pltpu.VMEM((4, 8, 2, 16, 256), BF16),
            pltpu.VMEM((4, 2, 8, 16, 256), BF16),
            pltpu.VMEM((4, 7, 2, 16, 256), BF16),
            pltpu.VMEM((7, 8, 16, 256), BF16),
            pltpu.VMEM((4, 2, 2, 16, 256), BF16),
            pltpu.VMEM((2, 8, 16, 256), BF16),
            pltpu.VMEM((4, 2, 16, 256), BF16),
            pltpu.VMEM((8, 16, 256), BF16),
            pltpu.VMEM((7, 16, 256), BF16),
            pltpu.VMEM((7, 16, 256), BF16),
            pltpu.VMEM((16, 512), BF16),
            pltpu.VMEM((8, 16, 512), BF16),
            dma, dma((4,)), dma, dma((4,)),
            dma((4,)), dma((4,)), dma((4, 7)), dma((4, 7)), dma((7,)), dma((7,)),
            dma((2, 7)), dma((2, 7)), dma((2, 7)), dma((2, 7)),
        ],
        compiler_params=pltpu.CompilerParams(collective_id=0, has_side_effects=True),
    )(block_input, conv_weight, bn_gain, out_cotangent)


def local(block_input, conv_weight, bn_gain, out_cotangent, master_weight, velocity):
    gradient = summed_gradient(block_input, conv_weight, bn_gain, out_cotangent).reshape(32, 512)
    new_velocity = MOMENTUM * velocity + gradient + DECAY * master_weight
    new_weight = master_weight - RATE * new_velocity
    return (new_velocity, new_weight)


def solution(mesh):
    in_specs = (
        P(("node", "local"), None),
        P(),
        P(),
        P(("node", "local"), None),
        P("node", None),
        P("node", None),
    )
    out_specs = (P("node", None), P("node", None))
    return jax.shard_map(local, mesh=mesh, in_specs=in_specs, out_specs=out_specs, check_vma=False)
```
